128 devices in a mesh: grp: 4 (over x_lo, core), mz: 32 (over y, x_hi, z).
Axes of the slice: x: 4 (x_hi: 2, x_lo: 2; x = x_hi * 2 + x_lo), y: 4, z: 4, core: 2. Of those that a mesh axis runs over, the one named last changes fastest.
Arguments:
- intensities: float32 [512, 8, 131072], P('grp', None, 'mz'), as said below
- sample_start: float32 [512, 256], P('grp'), as said below
- scan_start: float32 [8, 256], replicated, as said below
- mass_start: float32 [131072, 256], P('mz'), as said below
Outputs:
- sample_factor: float32 [512, 256], P('grp')
- scan_factor: float32 [8, 256], replicated
- mass_factor: float32 [131072, 256], P('mz')
Inputs may be any that keep to these rules, and one draw needn't show every extreme that they name: Measured intensities of the cohort. `sample_start`: a starting estimate of the sample factor. `scan_start`: a starting estimate of the scan factor. `mass_start`: a starting estimate of the m/z factor.
All inputs are finite; a program needn't handle non-finite values.
Results may differ from the reference program's by a relative error of at most 0.0001.
Values sent between devices are 32-bit elements; how exact they have to be, the bound alone decides.
A program may use at most 128 MiB of HBM per device.

```python
import math
import jax
import jax.numpy as jnp
from jax import lax

RANK = 256
SCANS = 8
STEPS = 2
SAMPLES = 512
BINS = 131072


def truth_factor(key, height, code, rising):
    first, second = jax.random.split(jax.random.fold_in(key, code), 2)
    random_part = jax.random.normal(first, (height, RANK), jnp.float32)
    shared = jax.random.normal(second, (height, 1), jnp.float32)
    slope = 2.0
    factor = random_part + shared
    if rising:
        position = jnp.arange(height, dtype=jnp.float32) / (height - 1.0)
        factor = factor * jnp.sqrt(1.0 + slope * position)[:, None]
    return factor


def perturbed(key, truth, code):
    noise_key = jax.random.fold_in(key, code)
    noise = 0.25 * jax.random.normal(noise_key, truth.shape, jnp.float32)
    return truth * (1.0 + noise)


def draw_intensities(key, part):
    sample_true = truth_factor(key, SAMPLES, 11, True)
    scan_true = truth_factor(key, SCANS, 23, False)
    mass_true = truth_factor(key, BINS, 37, True)
    khatri = (sample_true[:, None, :] * scan_true[None, :, :]).reshape(SAMPLES * SCANS, RANK)
    planted = jnp.dot(khatri, mass_true.T, precision=lax.Precision.HIGHEST, preferred_element_type=jnp.float32)
    noise = jax.random.normal(jax.random.fold_in(key, 53), (SAMPLES * SCANS, BINS), jnp.float32) * math.sqrt(RANK)
    return (planted + noise).reshape(SAMPLES, SCANS, BINS)


def draw_sample_start(key, part):
    return perturbed(key, truth_factor(key, SAMPLES, 11, True), 61)


def draw_scan_start(key, part):
    return perturbed(key, truth_factor(key, SCANS, 23, False), 67)


def draw_mass_start(key, part):
    return perturbed(key, truth_factor(key, BINS, 37, True), 71)


def setup_inputs(seed: int = 0) -> dict:
    key_list = jax.random.split(jax.random.key(seed), 5)
    intensities = draw_intensities(jax.random.fold_in(key_list[4], 71), 0)
    sample_start = draw_sample_start(jax.random.fold_in(key_list[4], 71), 0)
    scan_start = draw_scan_start(jax.random.fold_in(key_list[4], 71), 0)
    mass_start = draw_mass_start(jax.random.fold_in(key_list[4], 71), 0)
    return dict(intensities=intensities, sample_start=sample_start, scan_start=scan_start, mass_start=mass_start)


precise = lax.Precision.HIGHEST

def frobenius(gram):
    return jnp.sqrt(jnp.sum(gram * gram) + 1e-12)

def reference(intensities, sample_start, scan_start, mass_start):
    factor_a = sample_start
    factor_b = scan_start
    factor_c = mass_start
    unfolded = intensities.reshape(SAMPLES * SCANS, BINS)
    for iteration in range(STEPS):
        gram_a = jnp.dot(factor_a.T, factor_a, precision=precise, preferred_element_type=jnp.float32)
        gram_b = jnp.dot(factor_b.T, factor_b, precision=precise, preferred_element_type=jnp.float32)
        gram_c = jnp.dot(factor_c.T, factor_c, precision=precise, preferred_element_type=jnp.float32)
        contracted = jnp.einsum('ijk,kr->ijr', intensities, factor_c, precision=precise)
        drive_a = jnp.einsum('ijr,jr->ir', contracted, factor_b, precision=precise)
        drive_b = jnp.einsum('ijr,ir->jr', contracted, factor_a, precision=precise)
        khatri_rao = (factor_a[:, None, :] * factor_b[None, :, :]).reshape(SAMPLES * SCANS, RANK)
        drive_c = lax.dot_general(unfolded, khatri_rao, (((0,), (0,)), ((), ())), precision=precise, preferred_element_type=jnp.float32)
        hessian_a = gram_b * gram_c
        hessian_b = gram_a * gram_c
        hessian_c = gram_a * gram_b
        new_a = factor_a - (jnp.dot(factor_a, hessian_a, precision=precise, preferred_element_type=jnp.float32) - drive_a) / frobenius(hessian_a)
        new_b = factor_b - (jnp.dot(factor_b, hessian_b, precision=precise, preferred_element_type=jnp.float32) - drive_b) / frobenius(hessian_b)
        new_c = factor_c - (jnp.dot(factor_c, hessian_c, precision=precise, preferred_element_type=jnp.float32) - drive_c) / frobenius(hessian_c)
        factor_a, factor_b, factor_c = (new_a, new_b, new_c)
    return (factor_a, factor_b, factor_c)
```

```python
import functools

import jax
import jax.numpy as jnp
from jax import lax
from jax.experimental import pallas as pl
from jax.experimental.pallas import tpu as pltpu
from jax.sharding import PartitionSpec as P

MESH = pl.DeviceIdType.MESH
F32 = jnp.float32
BF16 = jnp.bfloat16
STEPS = 2
RANK = 256
SCANS = 8
ROWS = 128
BINS = 4096
CHUNKS = 16
WIDE = BINS // CHUNKS
HALF = WIDE // 2
FIRST = 8
SECOND = 10
THIRD = 10
PIECE = 72


def split(x):
    high = x.astype(BF16)
    return high, (x - high.astype(F32)).astype(BF16)


def contract(a, b, i, j, precision=None):
    return lax.dot_general(
        a, b, (((i,), (j,)), ((), ())), precision=precision, preferred_element_type=F32
    )


def contract3(a, b, i, j):
    return contract(a[0], b[0], i, j) + (contract(a[0], b[1], i, j) + contract(a[1], b[0], i, j))


def exact(a, b, i, j):
    return contract(a, b, i, j, lax.Precision.HIGHEST)


def inverse_norm(gram):
    return 1.0 / jnp.sqrt(jnp.sum(gram * gram) + 1e-12)


def kernel(
    t_hbm, a0, b0, c_hbm, out_a, out_b, out_c,
    t, c0, c1, c2, part, from_sib, from_cp, y, krh, krl, gram, a1, b1,
    pc, pa, ma, grama, pa_in, pa_sum, pa_cp, mb_out, mb_in,
    pieces, z_in, y_in, x_out, x_in, mbx_in, ag_in, half_out, half_in,
    t_sem, c_sem, o_sem, sib_s, sib_r, cp_s, cp_r, c1_s, c1_r, c2_s, c2_r, few_s, few_r,
):
    g = lax.axis_index("grp")
    m = lax.axis_index("mz")
    core = lax.rem(g, 2)
    z = lax.rem(m, 4)
    hi = lax.rem(m // 4, 2)
    yy = m // 8
    g_sib = g + 1 - 2 * core
    g_cp = lax.rem(g + 2, 4)
    m_x = m + 4 - 8 * hi
    sib, cp, xp, dg = (g_sib, m), (g_cp, m), (g, m_x), (g_cp, m_x)
    z_to = [(g, m - z + lax.rem(z + k, 4)) for k in (1, 2, 3)]
    y_to = [(g, m + 8 * (lax.rem(yy + k, 4) - yy)) for k in (1, 2, 3)]

    def load_t(i):
        cols = pl.ds(pl.multiple_of(i * WIDE, WIDE), WIDE)
        return pltpu.make_async_copy(t_hbm.at[:, cols], t.at[:, cols], t_sem.at[i])

    load_c = pltpu.make_async_copy(c_hbm, c0, c_sem)
    for i in range(CHUNKS):
        load_t(i).start()
    load_c.start()

    partners = [sib, cp, xp, dg, *z_to, *y_to]
    barrier = pltpu.get_barrier_semaphore()
    for partner in partners:
        pl.semaphore_signal(barrier, inc=1, device_id=partner, device_id_type=MESH)

    def khatri_rao(a, b):
        product = (a[:, None, :] * b[None, :, :]).reshape(ROWS * SCANS, RANK)
        krh[...], krl[...] = split(product)

    def remote(src, dst, send, recv, to):
        return pltpu.make_async_remote_copy(
            src_ref=src, dst_ref=dst, send_sem=send, recv_sem=recv, device_id=to, device_id_type=MESH
        )

    own = pl.ds(pl.multiple_of(core * HALF, HALF), HALF)
    other = pl.ds(pl.multiple_of((1 - core) * HALF, HALF), HALF)

    def to_sib(s, i):
        return remote(part.at[s, i, other], from_sib.at[s, i], sib_s.at[s, i], sib_r.at[s, i], sib)

    def to_cp(s, i):
        return remote(part.at[s, i, own], from_cp.at[s, i], cp_s.at[s, i], cp_r.at[s, i], cp)

    def chunk(i):
        return pl.ds(pl.multiple_of(i * WIDE, WIDE), WIDE)

    def own_rows(i):
        return pl.ds(pl.multiple_of(i * WIDE + core * HALF, HALF), HALF)

    def c1_to_sib(i):
        return remote(c1.at[own_rows(i)], c1.at[own_rows(i)], c1_s.at[i], c1_r.at[i], sib)

    def c2_to_sib(i):
        return remote(c2.at[i], out_c.at[own_rows(i)], c2_s.at[i], c2_r.at[i], sib)

    def c2_out(i):
        return pltpu.make_async_copy(c2.at[i], out_c.at[own_rows(i)], o_sem.at[i])

    def produce(s, i):
        part[s, i] = contract3(split(t[:, chunk(i)]), (krh[...], krl[...]), 0, 0)
        to_sib(s, i).start()

    def forward(s, i):
        to_sib(s, i).wait()
        part[s, i, own] += from_sib[s, i]
        to_cp(s, i).start()

    def run(s, first, last, wait_t=False):
        def body(i, carry):
            if wait_t:
                load_t(i).wait()
            produce(s, i)

            @pl.when(i > first)
            def _():
                forward(s, i - 1)

            return carry

        lax.fori_loop(first, last, body, 0)
        forward(s, last - 1)

    def accumulate(factor, i):
        rows = chunk(i)
        block = split(factor[rows, :])
        y[...] += contract3(split(t[:, rows]), block, 1, 0)
        mine = split(factor[rows, pl.ds(pl.multiple_of(core * 128, 128), 128)])
        gram[...] += contract3(mine, block, 0, 0)

    def update_c(s, i, source, hessian, scale):
        to_cp(s, i).wait()
        drive = part[s, i, own] + from_cp[s, i]
        old = source[own_rows(i), :]
        return old - (exact(old, hessian[...], 1, 0) - drive) * scale

    def small_pa(s, a):
        grama[...] = exact(a, a, 0, 0)
        theirs = pl.ds(pl.multiple_of((1 - core) * 128 + z * 32, 32), 32)
        return remote(grama.at[theirs], pa_in.at[s], few_s.at[s, 0], few_r.at[s, 0], sib)

    def small_pa_sum(s):
        mine = pl.ds(pl.multiple_of(core * 128 + z * 32, 32), 32)
        pa_sum[s] = grama[mine, :] + pa_in[s]
        return remote(pa_sum.at[s], pa_cp.at[s], few_s.at[s, 1], few_r.at[s, 1], cp)

    def small_mb(s, a):
        y3 = y[...].reshape(ROWS, SCANS, RANK)
        mb_out[s] = jnp.sum(y3 * a[:, None, :], axis=0)
        return remote(mb_out.at[s], mb_in.at[s], few_s.at[s, 2], few_r.at[s, 2], sib)

    def small_pieces(s, b, mb_copy):
        y3 = y[...].reshape(ROWS, SCANS, RANK)
        drive = jnp.sum(y3 * b[None, :, :], axis=1)
        mb_copy.wait()
        mb = mb_out[s] + mb_in[s]
        for p in range(4):
            pieces[s, p, 0:32, :] = drive[32 * p : 32 * p + 32]
            pieces[s, p, 32:64, :] = gram[32 * p : 32 * p + 32, :]
            pieces[s, p, 64:72, :] = mb
        copies = [
            remote(pieces.at[s, lax.rem(z + k, 4)], z_in.at[s, k], few_s.at[s, 2 + k], few_r.at[s, 2 + k], z_to[k - 1])
            for k in (1, 2, 3)
        ]
        for copy in copies:
            copy.start()
        z_in[s, 0] = pieces[s, z]
        return copies

    def ordered_sum(slots, s, me):
        total = slots[s, me]
        for other_one in (1, 2, 3):
            total = total + slots[s, lax.rem(me + 4 - other_one, 4)]
        return total

    def small_y(s):
        y_in[s, 0] = ordered_sum(z_in, s, z)
        copies = [
            remote(y_in.at[s, 0], y_in.at[s, k], few_s.at[s, 5 + k], few_r.at[s, 5 + k], y_to[k - 1]) for k in (1, 2, 3)
        ]
        for copy in copies:
            copy.start()
        return copies

    def small_x(s):
        x_out[s] = ordered_sum(y_in, s, yy)
        mb_rows = x_out.at[s, pl.ds(64, 8)]
        copies = [
            remote(x_out.at[s], x_in.at[s], few_s.at[s, 9], few_r.at[s, 9], xp),
            remote(mb_rows, mbx_in.at[s, 0], few_s.at[s, 10], few_r.at[s, 10], cp),
            remote(mb_rows, mbx_in.at[s, 1], few_s.at[s, 11], few_r.at[s, 11], dg),
        ]
        for copy in copies:
            copy.start()
        return copies

    def small_gather(s):
        ag_in[s, 0, 0:64, :] = x_out[s, 0:64, :] + x_in[s, 0:64, :]
        ag_in[s, 0, 64:96, :] = pa_sum[s] + pa_cp[s]
        copies = [
            remote(ag_in.at[s, 0], ag_in.at[s, k], few_s.at[s, 11 + k], few_r.at[s, 11 + k], z_to[k - 1])
            for k in (1, 2, 3)
        ]
        for copy in copies:
            copy.start()
        return copies

    def small_half(s):
        for p in range(4):
            k = lax.rem(z + 4 - p, 4)
            ma[32 * p : 32 * p + 32, :] = ag_in[s, k, 0:32, :]
            half_out[s, 32 * p : 32 * p + 32, :] = ag_in[s, k, 32:64, :]
            half_out[s, 128 + 32 * p : 128 + 32 * p + 32, :] = ag_in[s, k, 64:96, :]
        copy = remote(half_out.at[s], half_in.at[s], few_s.at[s, 15], few_r.at[s, 15], sib)
        copy.start()
        return copy

    def small_end(s, a, b):
        upper = pl.ds(pl.multiple_of(core * 128, 128), 128)
        lower = pl.ds(pl.multiple_of((1 - core) * 128, 128), 128)
        pc[upper, :] = half_out[s, 0:128, :]
        pc[lower, :] = half_in[s, 0:128, :]
        pa[upper, :] = half_out[s, 128:256, :]
        pa[lower, :] = half_in[s, 128:256, :]
        pb = exact(b, b, 0, 0)
        mb = (x_out[s, 64:72, :] + mbx_in[s, 0]) + (x_in[s, 64:72, :] + mbx_in[s, 1])
        hessian_a = pb * pc[...]
        hessian_b = pa[...] * pc[...]
        new_a = a - (exact(a, hessian_a, 1, 0) - ma[...]) * inverse_norm(hessian_a)
        new_b = b - (exact(b, hessian_b, 1, 0) - mb) * inverse_norm(hessian_b)
        hessian_c = pa[...] * pb
        scale = inverse_norm(hessian_c)
        pa[...] = hessian_c
        return new_a, new_b, scale

    def wait(copies):
        for copy in copies:
            copy.wait()

    khatri_rao(a0[...], b0[...])
    pl.semaphore_wait(barrier, len(partners))

    pa_copy = small_pa(0, a0[...])
    pa_copy.start()
    run(0, 0, 1, True)
    pa_copy.wait()
    pa_copy = small_pa_sum(0)
    pa_copy.start()
    run(0, 1, FIRST, True)
    load_c.wait()
    y[...] = jnp.zeros_like(y)
    gram[...] = jnp.zeros_like(gram)

    def first_y(i, carry):
        @pl.when(i >= FIRST)
        def _():
            load_t(i).wait()

        accumulate(c0, i)
        return carry

    lax.fori_loop(0, CHUNKS, first_y, 0)
    mb_copy = small_mb(0, a0[...])
    mb_copy.start()
    copies = small_pieces(0, b0[...], mb_copy)
    run(0, FIRST, SECOND)
    wait(copies)
    copies = small_y(0)
    wait(copies)
    copies = small_x(0)
    run(0, SECOND, CHUNKS)
    wait(copies)
    pa_copy.wait()
    copies = small_gather(0)
    wait(copies)
    copy = small_half(0)
    copy.wait()
    new_a, new_b, scale = small_end(0, a0[...], b0[...])
    a1[...] = new_a
    b1[...] = new_b
    khatri_rao(new_a, new_b)

    pa_copy = small_pa(1, new_a)
    pa_copy.start()
    run(1, 0, THIRD)
    pa_copy.wait()
    y[...] = jnp.zeros_like(y)
    gram[...] = jnp.zeros_like(gram)

    def second_y(i, carry):
        @pl.when(i < CHUNKS)
        def _():
            c1[own_rows(i), :] = update_c(0, i, c0, pa, scale)
            c1_to_sib(i).start()

        @pl.when(i > 0)
        def _():
            c1_to_sib(i - 1).wait()
            accumulate(c1, i - 1)

        return carry

    lax.fori_loop(0, CHUNKS + 1, second_y, 0)
    mb_copy = small_mb(1, a1[...])
    mb_copy.start()
    copies = small_pieces(1, b1[...], mb_copy)
    wait(copies)
    copies = small_y(1)
    wait(copies)
    pa_copy = small_pa_sum(1)
    pa_copy.start()
    copies = small_x(1)
    run(1, THIRD, CHUNKS)
    wait(copies)
    pa_copy.wait()
    copies = small_gather(1)
    wait(copies)
    copy = small_half(1)
    copy.wait()
    new_a, new_b, scale = small_end(1, a1[...], b1[...])
    out_a[...] = new_a
    out_b[...] = new_b

    def last_c(i, carry):
        c2[i] = update_c(1, i, c1, pa, scale)
        c2_to_sib(i).start()
        c2_out(i).start()
        return carry

    lax.fori_loop(0, CHUNKS, last_c, 0)

    def finish(i, carry):
        c2_to_sib(i).wait()
        c2_out(i).wait()
        return carry

    lax.fori_loop(0, CHUNKS, finish, 0)


def local(intensities, sample_start, scan_start, mass_start):
    unfolded = intensities.reshape(ROWS * SCANS, BINS)
    vmem = pl.BlockSpec(memory_space=pltpu.VMEM)
    anywhere = pl.BlockSpec(memory_space=pl.ANY)
    dma = pltpu.SemaphoreType.DMA
    return pl.pallas_call(
        kernel,
        out_shape=(
            jax.ShapeDtypeStruct((ROWS, RANK), F32),
            jax.ShapeDtypeStruct((SCANS, RANK), F32),
            jax.ShapeDtypeStruct((BINS, RANK), F32),
        ),
        in_specs=[anywhere, vmem, vmem, anywhere],
        out_specs=(vmem, vmem, anywhere),
        scratch_shapes=[
            pltpu.VMEM((ROWS * SCANS, BINS), F32),
            pltpu.VMEM((BINS, RANK), F32),
            pltpu.VMEM((BINS, RANK), F32),
            pltpu.VMEM((CHUNKS, HALF, RANK), F32),
            pltpu.VMEM((STEPS, CHUNKS, WIDE, RANK), F32),
            pltpu.VMEM((STEPS, CHUNKS, HALF, RANK), F32),
            pltpu.VMEM((STEPS, CHUNKS, HALF, RANK), F32),
            pltpu.VMEM((ROWS * SCANS, RANK), F32),
            pltpu.VMEM((ROWS * SCANS, RANK), BF16),
            pltpu.VMEM((ROWS * SCANS, RANK), BF16),
            pltpu.VMEM((128, RANK), F32),
            pltpu.VMEM((ROWS, RANK), F32),
            pltpu.VMEM((SCANS, RANK), F32),
            pltpu.VMEM((RANK, RANK), F32),
            pltpu.VMEM((RANK, RANK), F32),
            pltpu.VMEM((ROWS, RANK), F32),
            pltpu.VMEM((RANK, RANK), F32),
            pltpu.VMEM((STEPS, 32, RANK), F32),
            pltpu.VMEM((STEPS, 32, RANK), F32),
            pltpu.VMEM((STEPS, 32, RANK), F32),
            pltpu.VMEM((STEPS, 8, RANK), F32),
            pltpu.VMEM((STEPS, 8, RANK), F32),
            pltpu.VMEM((STEPS, 4, PIECE, RANK), F32),
            pltpu.VMEM((STEPS, 4, PIECE, RANK), F32),
            pltpu.VMEM((STEPS, 4, PIECE, RANK), F32),
            pltpu.VMEM((STEPS, PIECE, RANK), F32),
            pltpu.VMEM((STEPS, PIECE, RANK), F32),
            pltpu.VMEM((STEPS, 2, 8, RANK), F32),
            pltpu.VMEM((STEPS, 4, 96, RANK), F32),
            pltpu.VMEM((STEPS, 256, RANK), F32),
            pltpu.VMEM((STEPS, 256, RANK), F32),
            dma((CHUNKS,)),
            dma(()),
            dma((CHUNKS,)),
            dma((STEPS, CHUNKS)),
            dma((STEPS, CHUNKS)),
            dma((STEPS, CHUNKS)),
            dma((STEPS, CHUNKS)),
            dma((CHUNKS,)),
            dma((CHUNKS,)),
            dma((CHUNKS,)),
            dma((CHUNKS,)),
            dma((STEPS, 16)),
            dma((STEPS, 16)),
        ],
        compiler_params=pltpu.CompilerParams(
            collective_id=3, has_side_effects=True, vmem_limit_bytes=60 * 1024 * 1024
        ),
    )(unfolded, sample_start, scan_start, mass_start)


def solution(mesh):
    placed = (P("grp", None, "mz"), P("grp", None), P(), P("mz", None))
    return jax.shard_map(
        local,
        mesh=mesh,
        in_specs=placed,
        out_specs=(P("grp", None), P(), P("mz", None)),
        check_vma=False,
    )
```

```python
import functools

import jax
import jax.numpy as jnp
from jax import lax
from jax.experimental import pallas as pl
from jax.experimental.pallas import tpu as pltpu
from jax.sharding import PartitionSpec as P

MESH = pl.DeviceIdType.MESH
F32 = jnp.float32
BF16 = jnp.bfloat16
STEPS = 2
RANK = 256
SCANS = 8
ROWS = 128
BINS = 4096
CHUNKS = 8
WIDE = BINS // CHUNKS
HALF = WIDE // 2
FIRST = 4
SECOND = 5
THIRD = 4
TAKEN_Z, TAKEN_Y, TAKEN_X, TAKEN = 0, 2, 4, 5
PIECE = 72


def split(x):
    high = x.astype(BF16)
    return high, (x - high.astype(F32)).astype(BF16)


def contract(a, b, i, j, precision=None):
    return lax.dot_general(
        a, b, (((i,), (j,)), ((), ())), precision=precision, preferred_element_type=F32
    )


def contract3(a, b, i, j):
    return contract(a[0], b[0], i, j) + (contract(a[0], b[1], i, j) + contract(a[1], b[0], i, j))


def exact(a, b, i, j):
    return contract(a, b, i, j, lax.Precision.HIGHEST)


def inverse_norm(gram):
    return 1.0 / jnp.sqrt(jnp.sum(gram * gram) + 1e-12)


def kernel(
    t_hbm, a_hbm, b_hbm, c_hbm, out_a, out_b, out_c,
    a0, b0, t, c0, c1, part, from_sib, from_cp, y, krh, krl, gram, a1, b1,
    pc, pa, hc, ma, grama, pa_in, pa_sum, pa_cp, pa_ag, pa_half_out, pa_half_in, mb_out, mb_in,
    pieces, z_in, y_in, x_out, x_in, mbx_in, ag_in, half_out, half_in,
    t_sem, c_sem, sib_s, sib_r, cp_s, cp_r, c1_s, c1_r, c2_s, c2_r, few_s, few_r,
):
    g = lax.axis_index("grp")
    m = lax.axis_index("mz")
    core = lax.rem(g, 2)
    z = lax.rem(m, 4)
    hi = lax.rem(m // 4, 2)
    yy = m // 8
    g_sib = g + 1 - 2 * core
    g_cp = lax.rem(g + 2, 4)
    m_x = m + 4 - 8 * hi
    sib, cp, xp, dg = (g_sib, m), (g_cp, m), (g, m_x), (g_cp, m_x)
    z_to = [(g, m - z + lax.rem(z + k, 4)) for k in (1, 2, 3)]
    y_to = [(g, m + 8 * (lax.rem(yy + k, 4) - yy)) for k in (1, 2, 3)]

    partners = [sib, cp, xp, dg, *z_to, *y_to]
    barrier = pltpu.get_barrier_semaphore()
    for partner in partners:
        pl.semaphore_signal(barrier, inc=1, device_id=partner, device_id_type=MESH)

    def load_t(i):
        cols = pl.ds(pl.multiple_of(i * WIDE, WIDE), WIDE)
        return pltpu.make_async_copy(t_hbm.at[:, cols], t.at[:, cols], t_sem.at[i])

    load_c = pltpu.make_async_copy(c_hbm, c0, c_sem)
    load_a = pltpu.make_async_copy(a_hbm, a0, few_s.at[0, 20])
    load_b = pltpu.make_async_copy(b_hbm, b0, few_s.at[0, 21])
    load_a.start()
    load_b.start()
    load_t(0).start()

    def khatri_rao(a, b):
        product = (a[:, None, :] * b[None, :, :]).reshape(ROWS * SCANS, RANK)
        krh[...], krl[...] = split(product)

    def remote(src, dst, send, recv, to):
        return pltpu.make_async_remote_copy(
            src_ref=src, dst_ref=dst, send_sem=send, recv_sem=recv, device_id=to, device_id_type=MESH
        )

    own = pl.ds(pl.multiple_of(core * HALF, HALF), HALF)
    other = pl.ds(pl.multiple_of((1 - core) * HALF, HALF), HALF)

    def to_sib(s, i):
        return remote(part.at[s, i, other], from_sib.at[s, i], sib_s.at[s, i], sib_r.at[s, i], sib)

    def to_cp(s, i):
        return remote(part.at[s, i, own], from_cp.at[s, i], cp_s.at[s, i], cp_r.at[s, i], cp)

    def chunk(i):
        return pl.ds(pl.multiple_of(i * WIDE, WIDE), WIDE)

    def own_rows(i):
        return pl.ds(pl.multiple_of(i * WIDE + core * HALF, HALF), HALF)

    def c1_to_sib(i):
        return remote(c1.at[own_rows(i)], c1.at[own_rows(i)], c1_s.at[i], c1_r.at[i], sib)

    def c2_to_sib(i):
        return remote(out_c.at[own_rows(i)], out_c.at[own_rows(i)], c2_s.at[i], c2_r.at[i], sib)

    def produce(s, i):
        part[s, i] = contract3(split(t[:, chunk(i)]), (krh[...], krl[...]), 0, 0)
        to_sib(s, i).start()

    def prepare(s, i):
        to_sib(s, i).wait()
        part[s, i, own] += from_sib[s, i]

    def forward(s, i):
        prepare(s, i)
        to_cp(s, i).start()

    def run(s, first, last, wait_t=False, then=forward):
        def body(i, carry):
            if wait_t:
                load_t(i).wait()
            produce(s, i)

            @pl.when(i > first)
            def _():
                then(s, i - 1)

            return carry

        lax.fori_loop(first, last, body, 0)
        then(s, last - 1)

    def accumulate(factor, i):
        rows = chunk(i)
        block = split(factor[rows, :])
        y[...] += contract3(split(t[:, rows]), block, 1, 0)
        mine = split(factor[rows, pl.ds(pl.multiple_of(core * 128, 128), 128)])
        gram[...] += contract3(mine, block, 0, 0)

    def update_c(s, i, source, scale):
        to_cp(s, i).wait()
        drive = part[s, i, own] + from_cp[s, i]
        old = source[own_rows(i), :]
        return old - (exact(old, hc[s], 1, 0) - drive) * scale

    def small_pa(s, a):
        grama[...] = exact(a, a, 0, 0)
        theirs = pl.ds(pl.multiple_of((1 - core) * 128 + z * 32, 32), 32)
        return remote(grama.at[theirs], pa_in.at[s], few_s.at[s, 0], few_r.at[s, 0], sib)

    def small_pa_sum(s):
        mine = pl.ds(pl.multiple_of(core * 128 + z * 32, 32), 32)
        pa_sum[s] = grama[mine, :] + pa_in[s]
        return remote(pa_sum.at[s], pa_cp.at[s], few_s.at[s, 1], few_r.at[s, 1], cp)

    def small_pa_gather(s):
        pa_ag[s, 0] = pa_sum[s] + pa_cp[s]
        copies = [
            remote(pa_ag.at[s, 0], pa_ag.at[s, k], few_s.at[s, 15 + k], few_r.at[s, 15 + k], z_to[k - 1])
            for k in (1, 2, 3)
        ]
        for copy in copies:
            copy.start()
        return copies

    def small_pa_half(s):
        for p in range(4):
            pa_half_out[s, 32 * p : 32 * p + 32, :] = pa_ag[s, lax.rem(z + 4 - p, 4)]
        copy = remote(pa_half_out.at[s], pa_half_in.at[s], few_s.at[s, 19], few_r.at[s, 19], sib)
        copy.start()
        return copy

    upper = pl.ds(pl.multiple_of(core * 128, 128), 128)
    lower = pl.ds(pl.multiple_of((1 - core) * 128, 128), 128)

    def small_pa_end(s, b):
        pa[upper, :] = pa_half_out[s]
        pa[lower, :] = pa_half_in[s]
        hessian_c = pa[...] * exact(b, b, 0, 0)
        hc[s] = hessian_c
        return inverse_norm(hessian_c)

    def small_mb(s, a):
        y3 = y[...].reshape(ROWS, SCANS, RANK)
        mb_out[s] = jnp.sum(y3 * a[:, None, :], axis=0)
        return remote(mb_out.at[s], mb_in.at[s], few_s.at[s, 2], few_r.at[s, 2], sib)

    def small_pieces(s, b, mb_copy):
        y3 = y[...].reshape(ROWS, SCANS, RANK)
        drive = jnp.sum(y3 * b[None, :, :], axis=1)
        mb_copy.wait()
        mb = mb_out[s] + mb_in[s]
        for p in range(4):
            pieces[s, p, 0:32, :] = drive[32 * p : 32 * p + 32]
            pieces[s, p, 32:64, :] = gram[32 * p : 32 * p + 32, :]
            pieces[s, p, 64:72, :] = mb
        copies = [
            remote(pieces.at[s, lax.rem(z + k, 4)], z_in.at[s, k], few_s.at[s, 2 + k], few_r.at[s, 2 + k], z_to[k - 1])
            for k in (1, 2, 3)
        ]
        for copy in copies:
            copy.start()
        z_in[s, 0] = pieces[s, z]
        return copies

    def ordered_sum(slots, s, me):
        total = slots[s, me]
        for other_one in (1, 2, 3):
            total = total + slots[s, lax.rem(me + 4 - other_one, 4)]
        return total

    def small_y(s):
        y_in[s, 0] = ordered_sum(z_in, s, z)
        copies = [
            remote(y_in.at[s, 0], y_in.at[s, k], few_s.at[s, 5 + k], few_r.at[s, 5 + k], y_to[k - 1]) for k in (1, 2, 3)
        ]
        for copy in copies:
            copy.start()
        return copies

    def small_x(s):
        x_out[s] = ordered_sum(y_in, s, yy)
        mb_rows = x_out.at[s, pl.ds(64, 8)]
        copies = [
            remote(x_out.at[s], x_in.at[s], few_s.at[s, 9], few_r.at[s, 9], xp),
            remote(mb_rows, mbx_in.at[s, 0], few_s.at[s, 10], few_r.at[s, 10], cp),
            remote(mb_rows, mbx_in.at[s, 1], few_s.at[s, 11], few_r.at[s, 11], dg),
        ]
        for copy in copies:
            copy.start()
        return copies

    def small_gather(s):
        ag_in[s, 0] = x_out[s, 0:64, :] + x_in[s, 0:64, :]
        copies = [
            remote(ag_in.at[s, 0], ag_in.at[s, k], few_s.at[s, 11 + k], few_r.at[s, 11 + k], z_to[k - 1])
            for k in (1, 2, 3)
        ]
        for copy in copies:
            copy.start()
        return copies

    def small_half(s):
        for p in range(4):
            k = lax.rem(z + 4 - p, 4)
            ma[32 * p : 32 * p + 32, :] = ag_in[s, k, 0:32, :]
            half_out[s, 32 * p : 32 * p + 32, :] = ag_in[s, k, 32:64, :]
        copy = remote(half_out.at[s], half_in.at[s], few_s.at[s, 15], few_r.at[s, 15], sib)
        copy.start()
        return copy

    def small_end(s, a, b):
        pc[upper, :] = half_out[s]
        pc[lower, :] = half_in[s]
        pb = exact(b, b, 0, 0)
        mb = (x_out[s, 64:72, :] + mbx_in[s, 0]) + (x_in[s, 64:72, :] + mbx_in[s, 1])
        hessian_a = pb * pc[...]
        hessian_b = pa[...] * pc[...]
        new_a = a - (exact(a, hessian_a, 1, 0) - ma[...]) * inverse_norm(hessian_a)
        new_b = b - (exact(b, hessian_b, 1, 0) - mb) * inverse_norm(hessian_b)
        return new_a, new_b

    def wait(copies):
        for copy in copies:
            copy.wait()

    load_a.wait()
    load_b.wait()
    khatri_rao(a0[...], b0[...])
    pl.semaphore_wait(barrier, len(partners))

    def clear():
        y[...] = jnp.zeros_like(y)
        gram[...] = jnp.zeros_like(gram)

    def take(first, last, scale):
        def body(i, carry):
            c1[own_rows(i), :] = update_c(0, i, c0, scale)
            c1_to_sib(i).start()

            @pl.when(i > first)
            def _():
                c1_to_sib(i - 1).wait()
                accumulate(c1, i - 1)

            return carry

        if last > first:
            lax.fori_loop(first, last, body, 0)
            c1_to_sib(last - 1).wait()
            accumulate(c1, last - 1)

    pa_copy = small_pa(0, a0[...])
    pa_copy.start()
    load_t(0).wait()
    for i in range(1, CHUNKS):
        load_t(i).start()
    load_c.start()
    produce(0, 0)
    pa_copy.wait()
    pa_copy = small_pa_sum(0)
    pa_copy.start()
    forward(0, 0)
    run(0, 1, FIRST, True)
    pa_copy.wait()
    pa_copies = small_pa_gather(0)
    load_c.wait()
    clear()

    def first_y(i, carry):
        @pl.when(i >= FIRST)
        def _():
            load_t(i).wait()

        accumulate(c0, i)
        return carry

    lax.fori_loop(0, CHUNKS, first_y, 0)
    wait(pa_copies)
    pa_copy = small_pa_half(0)
    mb_copy = small_mb(0, a0[...])
    mb_copy.start()
    copies = small_pieces(0, b0[...], mb_copy)
    run(0, FIRST, SECOND)
    pa_copy.wait()
    scale = small_pa_end(0, b0[...])
    clear()
    take(TAKEN_Z, TAKEN_Y, scale)
    wait(copies)
    copies = small_y(0)
    take(TAKEN_Y, TAKEN_X, scale)
    wait(copies)
    copies = small_x(0)
    run(0, SECOND, CHUNKS)
    wait(copies)
    copies = small_gather(0)
    take(TAKEN_X, TAKEN, scale)
    wait(copies)
    copy = small_half(0)
    copy.wait()
    new_a, new_b = small_end(0, a0[...], b0[...])
    a1[...] = new_a
    b1[...] = new_b
    khatri_rao(new_a, new_b)

    pa_copy = small_pa(1, new_a)
    pa_copy.start()
    produce(1, 0)
    pa_copy.wait()
    pa_copy = small_pa_sum(1)
    pa_copy.start()
    forward(1, 0)
    run(1, 1, THIRD)
    take(TAKEN, CHUNKS, scale)
    pa_copy.wait()
    pa_copies = small_pa_gather(1)
    mb_copy = small_mb(1, a1[...])
    mb_copy.start()
    copies = small_pieces(1, b1[...], mb_copy)
    run(1, THIRD, CHUNKS - 2, then=prepare)
    wait(pa_copies)
    pa_copy = small_pa_half(1)
    wait(copies)
    copies = small_y(1)
    run(1, CHUNKS - 2, CHUNKS, then=prepare)
    pa_copy.wait()
    scale = small_pa_end(1, b1[...])
    wait(copies)
    copies = small_x(1)
    for i in range(THIRD, CHUNKS):
        to_cp(1, i).start()

    def last_c(i, carry):
        out_c[own_rows(i), :] = update_c(1, i, c1, scale)
        c2_to_sib(i).start()
        return carry

    lax.fori_loop(0, 2, last_c, 0)
    wait(copies)
    copies = small_gather(1)
    lax.fori_loop(2, 3, last_c, 0)
    wait(copies)
    copy = small_half(1)
    copy.wait()
    new_a, new_b = small_end(1, a1[...], b1[...])
    out_a[...] = new_a
    out_b[...] = new_b
    lax.fori_loop(3, CHUNKS, last_c, 0)

    def finish(i, carry):
        c2_to_sib(i).wait()
        return carry

    lax.fori_loop(0, CHUNKS, finish, 0)


def local(intensities, sample_start, scan_start, mass_start):
    unfolded = intensities.reshape(ROWS * SCANS, BINS)
    vmem = pl.BlockSpec(memory_space=pltpu.VMEM)
    anywhere = pl.BlockSpec(memory_space=pl.ANY)
    dma = pltpu.SemaphoreType.DMA
    return pl.pallas_call(
        kernel,
        out_shape=(
            pltpu.VMEM((ROWS, RANK), F32),
            pltpu.VMEM((SCANS, RANK), F32),
            pltpu.VMEM((BINS, RANK), F32),
        ),
        in_specs=[pl.BlockSpec(memory_space=pltpu.HBM)] * 4,
        out_specs=(vmem, vmem, vmem),
        scratch_shapes=[
            pltpu.VMEM((ROWS, RANK), F32),
            pltpu.VMEM((SCANS, RANK), F32),
            pltpu.VMEM((ROWS * SCANS, BINS), F32),
            pltpu.VMEM((BINS, RANK), F32),
            pltpu.VMEM((BINS, RANK), F32),
            pltpu.VMEM((STEPS, CHUNKS, WIDE, RANK), F32),
            pltpu.VMEM((STEPS, CHUNKS, HALF, RANK), F32),
            pltpu.VMEM((STEPS, CHUNKS, HALF, RANK), F32),
            pltpu.VMEM((ROWS * SCANS, RANK), F32),
            pltpu.VMEM((ROWS * SCANS, RANK), BF16),
            pltpu.VMEM((ROWS * SCANS, RANK), BF16),
            pltpu.VMEM((128, RANK), F32),
            pltpu.VMEM((ROWS, RANK), F32),
            pltpu.VMEM((SCANS, RANK), F32),
            pltpu.VMEM((RANK, RANK), F32),
            pltpu.VMEM((RANK, RANK), F32),
            pltpu.VMEM((STEPS, RANK, RANK), F32),
            pltpu.VMEM((ROWS, RANK), F32),
            pltpu.VMEM((RANK, RANK), F32),
            pltpu.VMEM((STEPS, 32, RANK), F32),
            pltpu.VMEM((STEPS, 32, RANK), F32),
            pltpu.VMEM((STEPS, 32, RANK), F32),
            pltpu.VMEM((STEPS, 4, 32, RANK), F32),
            pltpu.VMEM((STEPS, 128, RANK), F32),
            pltpu.VMEM((STEPS, 128, RANK), F32),
            pltpu.VMEM((STEPS, 8, RANK), F32),
            pltpu.VMEM((STEPS, 8, RANK), F32),
            pltpu.VMEM((STEPS, 4, PIECE, RANK), F32),
            pltpu.VMEM((STEPS, 4, PIECE, RANK), F32),
            pltpu.VMEM((STEPS, 4, PIECE, RANK), F32),
            pltpu.VMEM((STEPS, PIECE, RANK), F32),
            pltpu.VMEM((STEPS, PIECE, RANK), F32),
            pltpu.VMEM((STEPS, 2, 8, RANK), F32),
            pltpu.VMEM((STEPS, 4, 64, RANK), F32),
            pltpu.VMEM((STEPS, 128, RANK), F32),
            pltpu.VMEM((STEPS, 128, RANK), F32),
            dma((CHUNKS,)),
            dma(()),
            dma((STEPS, CHUNKS)),
            dma((STEPS, CHUNKS)),
            dma((STEPS, CHUNKS)),
            dma((STEPS, CHUNKS)),
            dma((CHUNKS,)),
            dma((CHUNKS,)),
            dma((CHUNKS,)),
            dma((CHUNKS,)),
            dma((STEPS, 22)),
            dma((STEPS, 22)),
        ],
        compiler_params=pltpu.CompilerParams(
            collective_id=3, has_side_effects=True, vmem_limit_bytes=54 * 1024 * 1024
        ),
    )(unfolded, sample_start, scan_start, mass_start)


def solution(mesh):
    placed = (P("grp", None, "mz"), P("grp", None), P(), P("mz", None))
    return jax.shard_map(
        local,
        mesh=mesh,
        in_specs=placed,
        out_specs=(P("grp", None), P(), P("mz", None)),
        check_vma=False,
    )
```

```python
import functools

import jax
import jax.numpy as jnp
from jax import lax
from jax.experimental import pallas as pl
from jax.experimental.pallas import tpu as pltpu
from jax.sharding import PartitionSpec as P

MESH = pl.DeviceIdType.MESH
F32 = jnp.float32
BF16 = jnp.bfloat16
STEPS = 2
RANK = 256
SCANS = 8
ROWS = 128
BINS = 4096
CHUNKS = 8
WIDE = BINS // CHUNKS
HALF = WIDE // 2
SPREAD = (False, True)
FIRST = 4
SECOND = 5
PA_CP, PA_HALF = 3, 7
THIRD = 4
TAKEN_Z, TAKEN_Y, TAKEN_X, TAKEN = 0, 2, 3, 3
PIECE = 72


def split(x):
    high = x.astype(BF16)
    return high, (x - high.astype(F32)).astype(BF16)


def contract(a, b, i, j, precision=None):
    return lax.dot_general(
        a, b, (((i,), (j,)), ((), ())), precision=precision, preferred_element_type=F32
    )


def contract3(a, b, i, j):
    return contract(a[0], b[0], i, j) + (contract(a[0], b[1], i, j) + contract(a[1], b[0], i, j))


def exact(a, b, i, j):
    return contract(a, b, i, j, lax.Precision.HIGHEST)


def inverse_norm(gram):
    return 1.0 / jnp.sqrt(jnp.sum(gram * gram) + 1e-12)


def kernel(
    t_hbm, a_hbm, b_hbm, c_hbm, out_a, out_b, out_c,
    a0, b0, t, c0, c1, part, from_sib, from_cp, y, krh, krl, gram, a1, b1,
    pc, pa, hc, ma, grama, pa_in, pa_sum, pa_cp, pa_ag, pa_half_out, pa_half_in, mb_out, mb_in,
    pieces, z_in, y_in, y_parts, y_some, y_ag, x_out, x_in, mbx_in, ag_in, half_out, half_in,
    t_sem, c_sem, sib_s, sib_r, cp_s, cp_r, c1_s, c1_r, c2_s, c2_r, few_s, few_r,
):
    g = lax.axis_index("grp")
    m = lax.axis_index("mz")
    core = lax.rem(g, 2)
    z = lax.rem(m, 4)
    hi = lax.rem(m // 4, 2)
    yy = m // 8
    g_sib = g + 1 - 2 * core
    g_cp = lax.rem(g + 2, 4)
    m_x = m + 4 - 8 * hi
    sib, cp, xp, dg = (g_sib, m), (g_cp, m), (g, m_x), (g_cp, m_x)
    z_to = [(g, m - z + lax.rem(z + k, 4)) for k in (1, 2, 3)]
    y_to = [(g, m + 8 * (lax.rem(yy + k, 4) - yy)) for k in (1, 2, 3)]

    partners = [sib, cp, xp, dg, *z_to, *y_to]
    barrier = pltpu.get_barrier_semaphore()
    for partner in partners:
        pl.semaphore_signal(barrier, inc=1, device_id=partner, device_id_type=MESH)

    def load_t(i):
        cols = pl.ds(pl.multiple_of(i * WIDE, WIDE), WIDE)
        return pltpu.make_async_copy(t_hbm.at[:, cols], t.at[:, cols], t_sem.at[i])

    load_c = pltpu.make_async_copy(c_hbm, c0, c_sem)
    load_a = pltpu.make_async_copy(a_hbm, a0, few_s.at[0, 20])
    load_b = pltpu.make_async_copy(b_hbm, b0, few_s.at[0, 21])
    load_a.start()
    load_b.start()
    load_t(0).start()

    def khatri_rao(a, b):
        product = (a[:, None, :] * b[None, :, :]).reshape(ROWS * SCANS, RANK)
        krh[...], krl[...] = split(product)

    def remote(src, dst, send, recv, to):
        return pltpu.make_async_remote_copy(
            src_ref=src, dst_ref=dst, send_sem=send, recv_sem=recv, device_id=to, device_id_type=MESH
        )

    own = pl.ds(pl.multiple_of(core * HALF, HALF), HALF)
    other = pl.ds(pl.multiple_of((1 - core) * HALF, HALF), HALF)

    def to_sib(s, i):
        return remote(part.at[s, i, other], from_sib.at[s, i], sib_s.at[s, i], sib_r.at[s, i], sib)

    def to_cp(s, i):
        return remote(part.at[s, i, own], from_cp.at[s, i], cp_s.at[s, i], cp_r.at[s, i], cp)

    def chunk(i):
        return pl.ds(pl.multiple_of(i * WIDE, WIDE), WIDE)

    def own_rows(i):
        return pl.ds(pl.multiple_of(i * WIDE + core * HALF, HALF), HALF)

    def c1_to_sib(i):
        return remote(c1.at[own_rows(i)], c1.at[own_rows(i)], c1_s.at[i], c1_r.at[i], sib)

    def c2_to_sib(i):
        return remote(out_c.at[own_rows(i)], out_c.at[own_rows(i)], c2_s.at[i], c2_r.at[i], sib)

    def produce(s, i):
        part[s, i] = contract3(split(t[:, chunk(i)]), (krh[...], krl[...]), 0, 0)
        to_sib(s, i).start()

    def prepare(s, i):
        to_sib(s, i).wait()
        part[s, i, own] += from_sib[s, i]

    def forward(s, i):
        prepare(s, i)
        to_cp(s, i).start()

    def run(s, first, last, wait_t=False, then=forward, also=None):
        def body(i, carry):
            if wait_t:
                load_t(i).wait()
            produce(s, i)
            if also is not None:
                also(i)

            @pl.when(i > first)
            def _():
                then(s, i - 1)

            return carry

        lax.fori_loop(first, last, body, 0)
        then(s, last - 1)

    def accumulate(factor, i):
        rows = chunk(i)
        block = split(factor[rows, :])
        y[...] += contract3(split(t[:, rows]), block, 1, 0)
        mine = split(factor[rows, pl.ds(pl.multiple_of(core * 128, 128), 128)])
        gram[...] += contract3(mine, block, 0, 0)

    def update_c(s, i, source, scale):
        to_cp(s, i).wait()
        drive = part[s, i, own] + from_cp[s, i]
        old = source[own_rows(i), :]
        return old - (exact(old, hc[s], 1, 0) - drive) * scale

    def small_pa(s, a):
        grama[...] = exact(a, a, 0, 0)
        theirs = pl.ds(pl.multiple_of((1 - core) * 128 + z * 32, 32), 32)
        return remote(grama.at[theirs], pa_in.at[s], few_s.at[s, 0], few_r.at[s, 0], sib)

    def small_pa_sum(s):
        mine = pl.ds(pl.multiple_of(core * 128 + z * 32, 32), 32)
        pa_sum[s] = grama[mine, :] + pa_in[s]
        return remote(pa_sum.at[s], pa_cp.at[s], few_s.at[s, 1], few_r.at[s, 1], cp)

    def pa_gather_copies(s):
        return [
            remote(pa_ag.at[s, 0], pa_ag.at[s, k], few_s.at[s, 15 + k], few_r.at[s, 15 + k], z_to[k - 1])
            for k in (1, 2, 3)
        ]

    def small_pa_gather(s):
        pa_ag[s, 0] = pa_sum[s] + pa_cp[s]
        copies = pa_gather_copies(s)
        for copy in copies:
            copy.start()
        return copies

    def small_pa_half(s):
        for p in range(4):
            pa_half_out[s, 32 * p : 32 * p + 32, :] = pa_ag[s, lax.rem(z + 4 - p, 4)]
        copy = remote(pa_half_out.at[s], pa_half_in.at[s], few_s.at[s, 19], few_r.at[s, 19], sib)
        copy.start()
        return copy

    upper = pl.ds(pl.multiple_of(core * 128, 128), 128)
    lower = pl.ds(pl.multiple_of((1 - core) * 128, 128), 128)

    def small_pa_end(s, b):
        pa[upper, :] = pa_half_out[s]
        pa[lower, :] = pa_half_in[s]
        hessian_c = pa[...] * exact(b, b, 0, 0)
        hc[s] = hessian_c
        return inverse_norm(hessian_c)

    def small_mb(s, a):
        y3 = y[...].reshape(ROWS, SCANS, RANK)
        mb_out[s] = jnp.sum(y3 * a[:, None, :], axis=0)
        return remote(mb_out.at[s], mb_in.at[s], few_s.at[s, 2], few_r.at[s, 2], sib)

    def small_pieces(s, b, mb_copy):
        y3 = y[...].reshape(ROWS, SCANS, RANK)
        drive = jnp.sum(y3 * b[None, :, :], axis=1)
        mb_copy.wait()
        mb = mb_out[s] + mb_in[s]
        for p in range(4):
            pieces[s, p, 0:32, :] = drive[32 * p : 32 * p + 32]
            pieces[s, p, 32:64, :] = gram[32 * p : 32 * p + 32, :]
            pieces[s, p, 64:72, :] = mb
        copies = [
            remote(pieces.at[s, lax.rem(z + k, 4)], z_in.at[s, k], few_s.at[s, 2 + k], few_r.at[s, 2 + k], z_to[k - 1])
            for k in (1, 2, 3)
        ]
        for copy in copies:
            copy.start()
        z_in[s, 0] = pieces[s, z]
        return copies

    def ordered_sum(slots, s, me):
        total = slots[s, me]
        for other_one in (1, 2, 3):
            total = total + slots[s, lax.rem(me + 4 - other_one, 4)]
        return total

    def small_y(s):
        total = ordered_sum(z_in, s, z)
        if SPREAD[s]:
            for p in range(4):
                y_parts[s, p, 0:8, :] = total[8 * p : 8 * p + 8]
                y_parts[s, p, 8:16, :] = total[32 + 8 * p : 40 + 8 * p]
                y_parts[s, p, 16:24, :] = total[64:72]
            y_some[s, 0] = y_parts[s, yy]
            copies = [
                remote(
                    y_parts.at[s, lax.rem(yy + k, 4)], y_some.at[s, k], few_s.at[s, 5 + k], few_r.at[s, 5 + k], y_to[k - 1]
                )
                for k in (1, 2, 3)
            ]
            for copy in copies:
                copy.start()
            return copies
        y_in[s, 0] = total
        copies = [
            remote(y_in.at[s, 0], y_in.at[s, k], few_s.at[s, 5 + k], few_r.at[s, 5 + k], y_to[k - 1]) for k in (1, 2, 3)
        ]
        for copy in copies:
            copy.start()
        return copies

    def small_x(s):
        if SPREAD[s]:
            x_out[s, 48:72, :] = ordered_sum(y_some, s, yy)
            sent = pl.ds(48, 24)
        else:
            x_out[s] = ordered_sum(y_in, s, yy)
            sent = pl.ds(0, PIECE)
        mb_rows = x_out.at[s, pl.ds(64, 8)]
        copies = [
            remote(x_out.at[s, sent], x_in.at[s, sent], few_s.at[s, 9], few_r.at[s, 9], xp),
            remote(mb_rows, mbx_in.at[s, 0], few_s.at[s, 10], few_r.at[s, 10], cp),
            remote(mb_rows, mbx_in.at[s, 1], few_s.at[s, 11], few_r.at[s, 11], dg),
        ]
        for copy in copies:
            copy.start()
        return copies

    def small_spread(s):
        y_ag[s, 0] = x_out[s, 48:64, :] + x_in[s, 48:64, :]
        copies = [
            remote(y_ag.at[s, 0], y_ag.at[s, k], few_s.at[s, 21 + k], few_r.at[s, 21 + k], y_to[k - 1]) for k in (1, 2, 3)
        ]
        for copy in copies:
            copy.start()
        return copies

    def small_gather(s):
        if SPREAD[s]:
            for p in range(4):
                block = y_ag[s, lax.rem(yy + 4 - p, 4)]
                ag_in[s, 0, 8 * p : 8 * p + 8, :] = block[0:8]
                ag_in[s, 0, 32 + 8 * p : 40 + 8 * p, :] = block[8:16]
        else:
            ag_in[s, 0] = x_out[s, 0:64, :] + x_in[s, 0:64, :]
        copies = [
            remote(ag_in.at[s, 0], ag_in.at[s, k], few_s.at[s, 11 + k], few_r.at[s, 11 + k], z_to[k - 1])
            for k in (1, 2, 3)
        ]
        for copy in copies:
            copy.start()
        return copies

    def small_half(s):
        for p in range(4):
            k = lax.rem(z + 4 - p, 4)
            ma[32 * p : 32 * p + 32, :] = ag_in[s, k, 0:32, :]
            half_out[s, 32 * p : 32 * p + 32, :] = ag_in[s, k, 32:64, :]
        copy = remote(half_out.at[s], half_in.at[s], few_s.at[s, 15], few_r.at[s, 15], sib)
        copy.start()
        return copy

    def small_end(s, a, b):
        pc[upper, :] = half_out[s]
        pc[lower, :] = half_in[s]
        pb = exact(b, b, 0, 0)
        mb = (x_out[s, 64:72, :] + mbx_in[s, 0]) + (x_in[s, 64:72, :] + mbx_in[s, 1])
        hessian_a = pb * pc[...]
        hessian_b = pa[...] * pc[...]
        new_a = a - (exact(a, hessian_a, 1, 0) - ma[...]) * inverse_norm(hessian_a)
        new_b = b - (exact(b, hessian_b, 1, 0) - mb) * inverse_norm(hessian_b)
        return new_a, new_b

    def wait(copies):
        for copy in copies:
            copy.wait()

    load_a.wait()
    load_b.wait()
    khatri_rao(a0[...], b0[...])
    pl.semaphore_wait(barrier, len(partners))

    def clear():
        y[...] = jnp.zeros_like(y)
        gram[...] = jnp.zeros_like(gram)

    def take(first, last, scale):
        def body(i, carry):
            @pl.when(i < last)
            def _():
                c1[own_rows(i), :] = update_c(0, i, c0, scale)
                c1_to_sib(i).start()

            @pl.when(i > first)
            def _():
                c1_to_sib(i - 1).wait()
                accumulate(c1, i - 1)

            return carry

        lax.fori_loop(first, last + 1, body, 0)

    load_t(0).wait()
    for i in range(1, CHUNKS):
        load_t(i).start()
    load_c.start()
    produce(0, 0)
    pa_copy = small_pa(0, a0[...])
    pa_copy.start()
    forward(0, 0)

    def pa_on(i):
        @pl.when(i == 1)
        def _():
            pa_copy.wait()
            small_pa_sum(0).start()

    run(0, 1, FIRST, True, also=pa_on)
    load_c.wait()
    clear()

    def first_y(i, carry):
        @pl.when(i >= FIRST)
        def _():
            load_t(i).wait()

        accumulate(c0, i)

        @pl.when(i == PA_CP)
        def _():
            remote(pa_sum.at[0], pa_cp.at[0], few_s.at[0, 1], few_r.at[0, 1], cp).wait()
            small_pa_gather(0)

        @pl.when(i == PA_HALF)
        def _():
            wait(pa_gather_copies(0))
            small_pa_half(0)

        return carry

    lax.fori_loop(0, CHUNKS, first_y, 0)
    pa_copy = remote(pa_half_out.at[0], pa_half_in.at[0], few_s.at[0, 19], few_r.at[0, 19], sib)
    mb_copy = small_mb(0, a0[...])
    mb_copy.start()
    copies = small_pieces(0, b0[...], mb_copy)
    run(0, FIRST, SECOND)
    pa_copy.wait()
    scale = small_pa_end(0, b0[...])
    clear()
    take(TAKEN_Z, TAKEN_Y, scale)
    wait(copies)
    copies = small_y(0)
    take(TAKEN_Y, TAKEN_X, scale)
    wait(copies)
    copies = small_x(0)
    run(0, SECOND, CHUNKS)
    wait(copies)
    if SPREAD[0]:
        copies = small_spread(0)
        wait(copies)
    copies = small_gather(0)
    wait(copies)
    copy = small_half(0)
    copy.wait()
    new_a, new_b = small_end(0, a0[...], b0[...])
    a1[...] = new_a
    b1[...] = new_b
    khatri_rao(new_a, new_b)

    pa_copy = small_pa(1, new_a)
    pa_copy.start()
    produce(1, 0)
    pa_copy.wait()
    pa_copy = small_pa_sum(1)
    pa_copy.start()
    forward(1, 0)
    run(1, 1, THIRD)
    take(TAKEN, CHUNKS, scale)
    pa_copy.wait()
    pa_copies = small_pa_gather(1)
    mb_copy = small_mb(1, a1[...])
    mb_copy.start()
    copies = small_pieces(1, b1[...], mb_copy)
    run(1, THIRD, CHUNKS - 2, then=prepare)
    wait(pa_copies)
    pa_copy = small_pa_half(1)
    wait(copies)
    copies = small_y(1)
    run(1, CHUNKS - 2, CHUNKS, then=prepare)
    pa_copy.wait()
    scale = small_pa_end(1, b1[...])
    wait(copies)
    copies = small_x(1)
    for i in range(THIRD, CHUNKS):
        to_cp(1, i).start()

    def last_c(i, carry):
        out_c[own_rows(i), :] = update_c(1, i, c1, scale)
        c2_to_sib(i).start()
        return carry

    lax.fori_loop(0, 3, last_c, 0)
    wait(copies)
    if SPREAD[1]:
        copies = small_spread(1)
        wait(copies)
    copies = small_gather(1)
    wait(copies)
    copy = small_half(1)
    copy.wait()
    new_a, new_b = small_end(1, a1[...], b1[...])
    out_a[...] = new_a
    out_b[...] = new_b
    lax.fori_loop(3, CHUNKS, last_c, 0)

    def finish(i, carry):
        c2_to_sib(i).wait()
        return carry

    lax.fori_loop(0, CHUNKS, finish, 0)


def local(intensities, sample_start, scan_start, mass_start):
    unfolded = intensities.reshape(ROWS * SCANS, BINS)
    vmem = pl.BlockSpec(memory_space=pltpu.VMEM)
    anywhere = pl.BlockSpec(memory_space=pl.ANY)
    dma = pltpu.SemaphoreType.DMA
    return pl.pallas_call(
        kernel,
        out_shape=(
            pltpu.VMEM((ROWS, RANK), F32),
            pltpu.VMEM((SCANS, RANK), F32),
            pltpu.VMEM((BINS, RANK), F32),
        ),
        in_specs=[pl.BlockSpec(memory_space=pltpu.HBM)] * 4,
        out_specs=(vmem, vmem, vmem),
        scratch_shapes=[
            pltpu.VMEM((ROWS, RANK), F32),
            pltpu.VMEM((SCANS, RANK), F32),
            pltpu.VMEM((ROWS * SCANS, BINS), F32),
            pltpu.VMEM((BINS, RANK), F32),
            pltpu.VMEM((BINS, RANK), F32),
            pltpu.VMEM((STEPS, CHUNKS, WIDE, RANK), F32),
            pltpu.VMEM((STEPS, CHUNKS, HALF, RANK), F32),
            pltpu.VMEM((STEPS, CHUNKS, HALF, RANK), F32),
            pltpu.VMEM((ROWS * SCANS, RANK), F32),
            pltpu.VMEM((ROWS * SCANS, RANK), BF16),
            pltpu.VMEM((ROWS * SCANS, RANK), BF16),
            pltpu.VMEM((128, RANK), F32),
            pltpu.VMEM((ROWS, RANK), F32),
            pltpu.VMEM((SCANS, RANK), F32),
            pltpu.VMEM((RANK, RANK), F32),
            pltpu.VMEM((RANK, RANK), F32),
            pltpu.VMEM((STEPS, RANK, RANK), F32),
            pltpu.VMEM((ROWS, RANK), F32),
            pltpu.VMEM((RANK, RANK), F32),
            pltpu.VMEM((STEPS, 32, RANK), F32),
            pltpu.VMEM((STEPS, 32, RANK), F32),
            pltpu.VMEM((STEPS, 32, RANK), F32),
            pltpu.VMEM((STEPS, 4, 32, RANK), F32),
            pltpu.VMEM((STEPS, 128, RANK), F32),
            pltpu.VMEM((STEPS, 128, RANK), F32),
            pltpu.VMEM((STEPS, 8, RANK), F32),
            pltpu.VMEM((STEPS, 8, RANK), F32),
            pltpu.VMEM((STEPS, 4, PIECE, RANK), F32),
            pltpu.VMEM((STEPS, 4, PIECE, RANK), F32),
            pltpu.VMEM((STEPS, 4, PIECE, RANK), F32),
            pltpu.VMEM((STEPS, 4, 24, RANK), F32),
            pltpu.VMEM((STEPS, 4, 24, RANK), F32),
            pltpu.VMEM((STEPS, 4, 16, RANK), F32),
            pltpu.VMEM((STEPS, PIECE, RANK), F32),
            pltpu.VMEM((STEPS, PIECE, RANK), F32),
            pltpu.VMEM((STEPS, 2, 8, RANK), F32),
            pltpu.VMEM((STEPS, 4, 64, RANK), F32),
            pltpu.VMEM((STEPS, 128, RANK), F32),
            pltpu.VMEM((STEPS, 128, RANK), F32),
            dma((CHUNKS,)),
            dma(()),
            dma((STEPS, CHUNKS)),
            dma((STEPS, CHUNKS)),
            dma((STEPS, CHUNKS)),
            dma((STEPS, CHUNKS)),
            dma((CHUNKS,)),
            dma((CHUNKS,)),
            dma((CHUNKS,)),
            dma((CHUNKS,)),
            dma((STEPS, 26)),
            dma((STEPS, 26)),
        ],
        compiler_params=pltpu.CompilerParams(
            collective_id=3, has_side_effects=True, vmem_limit_bytes=55 * 1024 * 1024
        ),
    )(unfolded, sample_start, scan_start, mass_start)


def solution(mesh):
    placed = (P("grp", None, "mz"), P("grp", None), P(), P("mz", None))
    return jax.shard_map(
        local,
        mesh=mesh,
        in_specs=placed,
        out_specs=(P("grp", None), P(), P("mz", None)),
        check_vma=False,
    )
```

```python
import functools

import jax
import jax.numpy as jnp
from jax import lax
from jax.experimental import pallas as pl
from jax.experimental.pallas import tpu as pltpu
from jax.sharding import PartitionSpec as P

MESH = pl.DeviceIdType.MESH
F32 = jnp.float32
BF16 = jnp.bfloat16
STEPS = 2
RANK = 256
SCANS = 8
ROWS = 128
BINS = 4096
CHUNKS = 8
WIDE = BINS // CHUNKS
HALF = WIDE // 2
SPREAD = (False, True)
FIRST = 4
SECOND = 5
PA_CP, PA_HALF = 3, 7
THIRD = 4
TAKEN_Z, TAKEN_Y, TAKEN_X, TAKEN = 0, 2, 3, 3
PIECE = 72


def split(x):
    high = x.astype(BF16)
    return high, (x - high.astype(F32)).astype(BF16)


def contract(a, b, i, j, precision=None):
    return lax.dot_general(
        a, b, (((i,), (j,)), ((), ())), precision=precision, preferred_element_type=F32
    )


def contract3(a, b, i, j):
    return contract(a[0], b[0], i, j) + (contract(a[0], b[1], i, j) + contract(a[1], b[0], i, j))


def exact(a, b, i, j):
    return contract(a, b, i, j, lax.Precision.HIGHEST)


def inverse_norm(gram):
    return 1.0 / jnp.sqrt(jnp.sum(gram * gram) + 1e-12)


def kernel(
    t_hbm, a_hbm, b_hbm, c_hbm, out_a, out_b, out_c,
    a0, b0, t, c0, c1, part, from_sib, from_cp, y, krh, krl, gram, a1, b1,
    pc, pa, hc, ma, grama, pa_in, pa_sum, pa_cp, pa_ag, pa_half_out, pa_half_in, mb_out, mb_in,
    pieces, z_in, y_in, y_parts, y_some, y_ag, x_out, x_in, mbx_in, ag_in, half_out, half_in,
    t_sem, c_sem, sib_s, sib_r, cp_s, cp_r, c1_s, c1_r, c2_s, c2_r, few_s, few_r,
):
    g = lax.axis_index("grp")
    m = lax.axis_index("mz")
    core = lax.rem(g, 2)
    z = lax.rem(m, 4)
    hi = lax.rem(m // 4, 2)
    yy = m // 8
    g_sib = g + 1 - 2 * core
    g_cp = lax.rem(g + 2, 4)
    m_x = m + 4 - 8 * hi
    sib, cp, xp, dg = (g_sib, m), (g_cp, m), (g, m_x), (g_cp, m_x)
    z_to = [(g, m - z + lax.rem(z + k, 4)) for k in (1, 2, 3)]
    y_to = [(g, m + 8 * (lax.rem(yy + k, 4) - yy)) for k in (1, 2, 3)]

    partners = [sib, cp, xp, dg, *z_to, *y_to]
    barrier = pltpu.get_barrier_semaphore()
    for partner in partners:
        pl.semaphore_signal(barrier, inc=1, device_id=partner, device_id_type=MESH)

    def load_t(i):
        cols = pl.ds(pl.multiple_of(i * WIDE, WIDE), WIDE)
        return pltpu.make_async_copy(t_hbm.at[:, cols], t.at[:, cols], t_sem.at[i])

    load_c = pltpu.make_async_copy(c_hbm, c0, c_sem)
    load_a = pltpu.make_async_copy(a_hbm, a0, few_s.at[0, 20])
    load_b = pltpu.make_async_copy(b_hbm, b0, few_s.at[0, 21])
    load_a.start()
    load_b.start()
    load_t(0).start()

    def khatri_rao(a, b):
        product = (a[:, None, :] * b[None, :, :]).reshape(ROWS * SCANS, RANK)
        krh[...], krl[...] = split(product)

    def remote(src, dst, send, recv, to):
        return pltpu.make_async_remote_copy(
            src_ref=src, dst_ref=dst, send_sem=send, recv_sem=recv, device_id=to, device_id_type=MESH
        )

    own = pl.ds(pl.multiple_of(core * HALF, HALF), HALF)
    other = pl.ds(pl.multiple_of((1 - core) * HALF, HALF), HALF)

    def to_sib(s, i):
        return remote(part.at[s, i, other], from_sib.at[s, i], sib_s.at[s, i], sib_r.at[s, i], sib)

    def to_cp(s, i):
        return remote(part.at[s, i, own], from_cp.at[s, i], cp_s.at[s, i], cp_r.at[s, i], cp)

    def chunk(i):
        return pl.ds(pl.multiple_of(i * WIDE, WIDE), WIDE)

    def own_rows(i):
        return pl.ds(pl.multiple_of(i * WIDE + core * HALF, HALF), HALF)

    def c1_to_sib(i):
        return remote(c1.at[own_rows(i)], c1.at[own_rows(i)], c1_s.at[i], c1_r.at[i], sib)

    def c2_to_sib(i):
        return remote(out_c.at[own_rows(i)], out_c.at[own_rows(i)], c2_s.at[i], c2_r.at[i], sib)

    def produce(s, i):
        part[s, i] = contract3(split(t[:, chunk(i)]), (krh[...], krl[...]), 0, 0)
        to_sib(s, i).start()

    def prepare(s, i):
        to_sib(s, i).wait()
        part[s, i, own] += from_sib[s, i]

    def forward(s, i):
        prepare(s, i)
        to_cp(s, i).start()

    def run(s, first, last, wait_t=False, then=forward, also=None):
        def body(i, carry):
            if wait_t:
                load_t(i).wait()
            produce(s, i)
            if also is not None:
                also(i)

            @pl.when(i > first)
            def _():
                then(s, i - 1)

            return carry

        lax.fori_loop(first, last, body, 0)
        then(s, last - 1)

    def accumulate(factor, i):
        rows = chunk(i)
        block = split(factor[rows, :])
        y[...] += contract3(split(t[:, rows]), block, 1, 0)
        mine = split(factor[rows, pl.ds(pl.multiple_of(core * 128, 128), 128)])
        gram[...] += contract3(mine, block, 0, 0)

    def update_c(s, i, source, scale):
        to_cp(s, i).wait()
        drive = part[s, i, own] + from_cp[s, i]
        old = source[own_rows(i), :]
        return old - (exact(old, hc[s], 1, 0) - drive) * scale

    def small_pa(s, a):
        grama[...] = exact(a, a, 0, 0)
        theirs = pl.ds(pl.multiple_of((1 - core) * 128 + z * 32, 32), 32)
        return remote(grama.at[theirs], pa_in.at[s], few_s.at[s, 0], few_r.at[s, 0], sib)

    def small_pa_sum(s):
        mine = pl.ds(pl.multiple_of(core * 128 + z * 32, 32), 32)
        pa_sum[s] = grama[mine, :] + pa_in[s]
        return remote(pa_sum.at[s], pa_cp.at[s], few_s.at[s, 1], few_r.at[s, 1], cp)

    def pa_gather_copies(s):
        return [
            remote(pa_ag.at[s, 0], pa_ag.at[s, k], few_s.at[s, 15 + k], few_r.at[s, 15 + k], z_to[k - 1])
            for k in (1, 2, 3)
        ]

    def small_pa_gather(s):
        pa_ag[s, 0] = pa_sum[s] + pa_cp[s]
        copies = pa_gather_copies(s)
        for copy in copies:
            copy.start()
        return copies

    def small_pa_half(s):
        for p in range(4):
            pa_half_out[s, 32 * p : 32 * p + 32, :] = pa_ag[s, lax.rem(z + 4 - p, 4)]
        copy = remote(pa_half_out.at[s], pa_half_in.at[s], few_s.at[s, 19], few_r.at[s, 19], sib)
        copy.start()
        return copy

    upper = pl.ds(pl.multiple_of(core * 128, 128), 128)
    lower = pl.ds(pl.multiple_of((1 - core) * 128, 128), 128)

    def small_pa_end(s, b):
        pa[upper, :] = pa_half_out[s]
        pa[lower, :] = pa_half_in[s]
        hessian_c = pa[...] * exact(b, b, 0, 0)
        hc[s] = hessian_c
        return inverse_norm(hessian_c)

    def small_mb(s, a):
        y3 = y[...].reshape(ROWS, SCANS, RANK)
        mb_out[s] = jnp.sum(y3 * a[:, None, :], axis=0)
        return remote(mb_out.at[s], mb_in.at[s], few_s.at[s, 2], few_r.at[s, 2], sib)

    def small_pieces(s, b, mb_copy):
        y3 = y[...].reshape(ROWS, SCANS, RANK)
        drive = jnp.sum(y3 * b[None, :, :], axis=1)
        mb_copy.wait()
        mb = mb_out[s] + mb_in[s]
        for p in range(4):
            pieces[s, p, 0:32, :] = drive[32 * p : 32 * p + 32]
            pieces[s, p, 32:64, :] = gram[32 * p : 32 * p + 32, :]
            pieces[s, p, 64:72, :] = mb
        copies = [
            remote(pieces.at[s, lax.rem(z + k, 4)], z_in.at[s, k], few_s.at[s, 2 + k], few_r.at[s, 2 + k], z_to[k - 1])
            for k in (1, 2, 3)
        ]
        for copy in copies:
            copy.start()
        z_in[s, 0] = pieces[s, z]
        return copies

    def ordered_sum(slots, s, me):
        total = slots[s, me]
        for other_one in (1, 2, 3):
            total = total + slots[s, lax.rem(me + 4 - other_one, 4)]
        return total

    def small_y(s):
        total = ordered_sum(z_in, s, z)
        if SPREAD[s]:
            for p in range(4):
                y_parts[s, p, 0:8, :] = total[8 * p : 8 * p + 8]
                y_parts[s, p, 8:16, :] = total[32 + 8 * p : 40 + 8 * p]
                y_parts[s, p, 16:24, :] = total[64:72]
            y_some[s, 0] = y_parts[s, yy]
            copies = [
                remote(
                    y_parts.at[s, lax.rem(yy + k, 4)], y_some.at[s, k], few_s.at[s, 5 + k], few_r.at[s, 5 + k], y_to[k - 1]
                )
                for k in (1, 2, 3)
            ]
            for copy in copies:
                copy.start()
            return copies
        y_in[s, 0] = total
        copies = [
            remote(y_in.at[s, 0], y_in.at[s, k], few_s.at[s, 5 + k], few_r.at[s, 5 + k], y_to[k - 1]) for k in (1, 2, 3)
        ]
        for copy in copies:
            copy.start()
        return copies

    def small_x(s):
        if SPREAD[s]:
            x_out[s, 48:72, :] = ordered_sum(y_some, s, yy)
            sent = pl.ds(48, 24)
        else:
            x_out[s] = ordered_sum(y_in, s, yy)
            sent = pl.ds(0, PIECE)
        mb_rows = x_out.at[s, pl.ds(64, 8)]
        copies = [
            remote(x_out.at[s, sent], x_in.at[s, sent], few_s.at[s, 9], few_r.at[s, 9], xp),
            remote(mb_rows, mbx_in.at[s, 0], few_s.at[s, 10], few_r.at[s, 10], cp),
            remote(mb_rows, mbx_in.at[s, 1], few_s.at[s, 11], few_r.at[s, 11], dg),
        ]
        for copy in copies:
            copy.start()
        return copies

    def small_spread(s):
        y_ag[s, 0] = x_out[s, 48:64, :] + x_in[s, 48:64, :]
        copies = [
            remote(y_ag.at[s, 0], y_ag.at[s, k], few_s.at[s, 21 + k], few_r.at[s, 21 + k], y_to[k - 1]) for k in (1, 2, 3)
        ]
        for copy in copies:
            copy.start()
        return copies

    def small_gather(s):
        if SPREAD[s]:
            for p in range(4):
                block = y_ag[s, lax.rem(yy + 4 - p, 4)]
                ag_in[s, 0, 8 * p : 8 * p + 8, :] = block[0:8]
                ag_in[s, 0, 32 + 8 * p : 40 + 8 * p, :] = block[8:16]
        else:
            ag_in[s, 0] = x_out[s, 0:64, :] + x_in[s, 0:64, :]
        copies = [
            remote(ag_in.at[s, 0], ag_in.at[s, k], few_s.at[s, 11 + k], few_r.at[s, 11 + k], z_to[k - 1])
            for k in (1, 2, 3)
        ]
        for copy in copies:
            copy.start()
        return copies

    def small_half(s):
        for p in range(4):
            k = lax.rem(z + 4 - p, 4)
            ma[32 * p : 32 * p + 32, :] = ag_in[s, k, 0:32, :]
            half_out[s, 32 * p : 32 * p + 32, :] = ag_in[s, k, 32:64, :]
        copy = remote(half_out.at[s], half_in.at[s], few_s.at[s, 15], few_r.at[s, 15], sib)
        copy.start()
        return copy

    def small_end(s, a, b):
        pc[upper, :] = half_out[s]
        pc[lower, :] = half_in[s]
        pb = exact(b, b, 0, 0)
        mb = (x_out[s, 64:72, :] + mbx_in[s, 0]) + (x_in[s, 64:72, :] + mbx_in[s, 1])
        hessian_a = pb * pc[...]
        hessian_b = pa[...] * pc[...]
        new_a = a - (exact(a, hessian_a, 1, 0) - ma[...]) * inverse_norm(hessian_a)
        new_b = b - (exact(b, hessian_b, 1, 0) - mb) * inverse_norm(hessian_b)
        return new_a, new_b

    def wait(copies):
        for copy in copies:
            copy.wait()

    load_a.wait()
    load_b.wait()
    khatri_rao(a0[...], b0[...])
    pl.semaphore_wait(barrier, len(partners))

    def clear():
        y[...] = jnp.zeros_like(y)
        gram[...] = jnp.zeros_like(gram)

    def take(first, last, scale):
        def body(i, carry):
            @pl.when(i < last)
            def _():
                c1[own_rows(i), :] = update_c(0, i, c0, scale)
                c1_to_sib(i).start()

            @pl.when(i > first)
            def _():
                c1_to_sib(i - 1).wait()
                accumulate(c1, i - 1)

            return carry

        lax.fori_loop(first, last + 1, body, 0)

    load_t(0).wait()
    for i in range(1, CHUNKS):
        load_t(i).start()
    load_c.start()
    produce(0, 0)
    pa_copy = small_pa(0, a0[...])
    pa_copy.start()
    forward(0, 0)

    def pa_on(i):
        @pl.when(i == 1)
        def _():
            pa_copy.wait()
            small_pa_sum(0).start()

    run(0, 1, FIRST, True, also=pa_on)
    load_c.wait()
    clear()

    def first_y(i, carry):
        @pl.when(i >= FIRST)
        def _():
            load_t(i).wait()

        accumulate(c0, i)

        @pl.when(i == PA_CP)
        def _():
            remote(pa_sum.at[0], pa_cp.at[0], few_s.at[0, 1], few_r.at[0, 1], cp).wait()
            small_pa_gather(0)

        @pl.when(i == PA_HALF)
        def _():
            wait(pa_gather_copies(0))
            small_pa_half(0)

        return carry

    lax.fori_loop(0, CHUNKS, first_y, 0)
    pa_copy = remote(pa_half_out.at[0], pa_half_in.at[0], few_s.at[0, 19], few_r.at[0, 19], sib)
    mb_copy = small_mb(0, a0[...])
    mb_copy.start()
    copies = small_pieces(0, b0[...], mb_copy)
    run(0, FIRST, SECOND)
    pa_copy.wait()
    scale = small_pa_end(0, b0[...])
    clear()
    take(TAKEN_Z, TAKEN_Y, scale)
    wait(copies)
    copies = small_y(0)
    take(TAKEN_Y, TAKEN_X, scale)
    wait(copies)
    copies = small_x(0)
    run(0, SECOND, CHUNKS)
    wait(copies)
    if SPREAD[0]:
        copies = small_spread(0)
        wait(copies)
    copies = small_gather(0)
    wait(copies)
    copy = small_half(0)
    copy.wait()
    new_a, new_b = small_end(0, a0[...], b0[...])
    a1[...] = new_a
    b1[...] = new_b
    khatri_rao(new_a, new_b)

    produce(1, 0)
    pa_copy = small_pa(1, new_a)
    pa_copy.start()
    forward(1, 0)
    pa_copy.wait()
    pa_copy = small_pa_sum(1)
    pa_copy.start()
    run(1, 1, THIRD)
    take(TAKEN, CHUNKS, scale)
    pa_copy.wait()
    pa_copies = small_pa_gather(1)
    mb_copy = small_mb(1, a1[...])
    mb_copy.start()
    copies = small_pieces(1, b1[...], mb_copy)
    run(1, THIRD, CHUNKS - 2, then=prepare)
    wait(pa_copies)
    pa_copy = small_pa_half(1)
    wait(copies)
    copies = small_y(1)
    run(1, CHUNKS - 2, CHUNKS, then=prepare)
    pa_copy.wait()
    scale = small_pa_end(1, b1[...])
    wait(copies)
    copies = small_x(1)
    for i in range(THIRD, CHUNKS):
        to_cp(1, i).start()

    def last_c(i, carry):
        out_c[own_rows(i), :] = update_c(1, i, c1, scale)
        c2_to_sib(i).start()
        return carry

    lax.fori_loop(0, 3, last_c, 0)
    wait(copies)
    if SPREAD[1]:
        copies = small_spread(1)
        wait(copies)
    copies = small_gather(1)
    wait(copies)
    copy = small_half(1)
    copy.wait()
    new_a, new_b = small_end(1, a1[...], b1[...])
    out_a[...] = new_a
    out_b[...] = new_b
    lax.fori_loop(3, CHUNKS, last_c, 0)

    def finish(i, carry):
        c2_to_sib(i).wait()
        return carry

    lax.fori_loop(0, CHUNKS, finish, 0)


def local(intensities, sample_start, scan_start, mass_start):
    unfolded = intensities.reshape(ROWS * SCANS, BINS)
    vmem = pl.BlockSpec(memory_space=pltpu.VMEM)
    anywhere = pl.BlockSpec(memory_space=pl.ANY)
    dma = pltpu.SemaphoreType.DMA
    return pl.pallas_call(
        kernel,
        out_shape=(
            pltpu.VMEM((ROWS, RANK), F32),
            pltpu.VMEM((SCANS, RANK), F32),
            pltpu.VMEM((BINS, RANK), F32),
        ),
        in_specs=[pl.BlockSpec(memory_space=pltpu.HBM)] * 4,
        out_specs=(vmem, vmem, vmem),
        scratch_shapes=[
            pltpu.VMEM((ROWS, RANK), F32),
            pltpu.VMEM((SCANS, RANK), F32),
            pltpu.VMEM((ROWS * SCANS, BINS), F32),
            pltpu.VMEM((BINS, RANK), F32),
            pltpu.VMEM((BINS, RANK), F32),
            pltpu.VMEM((STEPS, CHUNKS, WIDE, RANK), F32),
            pltpu.VMEM((STEPS, CHUNKS, HALF, RANK), F32),
            pltpu.VMEM((STEPS, CHUNKS, HALF, RANK), F32),
            pltpu.VMEM((ROWS * SCANS, RANK), F32),
            pltpu.VMEM((ROWS * SCANS, RANK), BF16),
            pltpu.VMEM((ROWS * SCANS, RANK), BF16),
            pltpu.VMEM((128, RANK), F32),
            pltpu.VMEM((ROWS, RANK), F32),
            pltpu.VMEM((SCANS, RANK), F32),
            pltpu.VMEM((RANK, RANK), F32),
            pltpu.VMEM((RANK, RANK), F32),
            pltpu.VMEM((STEPS, RANK, RANK), F32),
            pltpu.VMEM((ROWS, RANK), F32),
            pltpu.VMEM((RANK, RANK), F32),
            pltpu.VMEM((STEPS, 32, RANK), F32),
            pltpu.VMEM((STEPS, 32, RANK), F32),
            pltpu.VMEM((STEPS, 32, RANK), F32),
            pltpu.VMEM((STEPS, 4, 32, RANK), F32),
            pltpu.VMEM((STEPS, 128, RANK), F32),
            pltpu.VMEM((STEPS, 128, RANK), F32),
            pltpu.VMEM((STEPS, 8, RANK), F32),
            pltpu.VMEM((STEPS, 8, RANK), F32),
            pltpu.VMEM((STEPS, 4, PIECE, RANK), F32),
            pltpu.VMEM((STEPS, 4, PIECE, RANK), F32),
            pltpu.VMEM((STEPS, 4, PIECE, RANK), F32),
            pltpu.VMEM((STEPS, 4, 24, RANK), F32),
            pltpu.VMEM((STEPS, 4, 24, RANK), F32),
            pltpu.VMEM((STEPS, 4, 16, RANK), F32),
            pltpu.VMEM((STEPS, PIECE, RANK), F32),
            pltpu.VMEM((STEPS, PIECE, RANK), F32),
            pltpu.VMEM((STEPS, 2, 8, RANK), F32),
            pltpu.VMEM((STEPS, 4, 64, RANK), F32),
            pltpu.VMEM((STEPS, 128, RANK), F32),
            pltpu.VMEM((STEPS, 128, RANK), F32),
            dma((CHUNKS,)),
            dma(()),
            dma((STEPS, CHUNKS)),
            dma((STEPS, CHUNKS)),
            dma((STEPS, CHUNKS)),
            dma((STEPS, CHUNKS)),
            dma((CHUNKS,)),
            dma((CHUNKS,)),
            dma((CHUNKS,)),
            dma((CHUNKS,)),
            dma((STEPS, 26)),
            dma((STEPS, 26)),
        ],
        compiler_params=pltpu.CompilerParams(
            collective_id=3, has_side_effects=True, vmem_limit_bytes=55 * 1024 * 1024
        ),
    )(unfolded, sample_start, scan_start, mass_start)


def solution(mesh):
    placed = (P("grp", None, "mz"), P("grp", None), P(), P("mz", None))
    return jax.shard_map(
        local,
        mesh=mesh,
        in_specs=placed,
        out_specs=(P("grp", None), P(), P("mz", None)),
        check_vma=False,
    )
```
